512 devices in a mesh: wide: 32 (over y_lo, z), narrow: 16 (over y_hi, x, core).
Axes of the slice: x: 4, y: 8 (y_hi: 2, y_lo: 4; y = y_hi * 4 + y_lo), z: 8, core: 2. Of those that a mesh axis runs over, the one named last changes fastest.
Arguments:
- amplitudes: float32 [32, 64, 256, 256], P('wide', 'narrow'), may hold values from -6 to 6
- driver: float32 [32, 64, 256, 256], P('wide', 'narrow'), may hold values from -15 to 15
- fit_vectors: float32 [64, 1024, 256], P('narrow', 'wide'), may hold values from -0.09375 to 0.09375
- ladder_factors: float32 [2, 256, 256], P(None, 'wide'), may hold values from -0.25 to 0.25
- row_energy: float32 [32], P('wide'), may hold values from -2 to -0.3
- occupied_energy: float32 [64], P('narrow'), may hold values from -2 to -0.3
- virtual_energy: float32 [256], replicated, may hold values from 0.5 to 3
Outputs:
- updated: float32 [32, 64, 256, 256], P('wide', 'narrow')
The draws below stay inside these ranges and needn't reach their ends.
All inputs are finite; a program needn't handle non-finite values.
Results may differ from the reference program's by a relative error of at most 0.0001.
Values sent between devices are 32-bit elements; how exact they have to be, the bound alone decides.
No kernel may reach another device: no remote copies, remote signals or barrier semaphores. Data moves between devices by JAX's collectives and lax.ppermute only.
A program may use at most 64 MiB of HBM per device.

```python
import jax
import jax.numpy as jnp
from jax import lax

O = 64
V = 256
NQ = 1024
NL = 2
ITERS = 2
NI = 32


def block_levels(own_key, dims, cuts, smallest, top_value):
    loudness = 1.0
    for dim, blocks in cuts:
        steps = jax.random.uniform(jax.random.fold_in(jax.random.fold_in(own_key, 6), dim), (blocks,), jnp.float32, smallest / len(cuts), top_value / len(cuts))
        loudness = loudness * jnp.repeat(jnp.exp(steps), dims[dim] // blocks).reshape((-1,) + (1,) * (len(dims) - 1 - dim))
    return loudness


def normal_values(key, shape, scale, most, cuts=(), held_as=jnp.bfloat16):
    values = jax.random.normal(key, shape, jnp.float32) * scale
    if len(cuts) > 0:
        values = block_levels(key, shape, cuts, -0.22, 0.18) * values
    return jnp.clip(values, min=-most, max=most).astype(held_as)


def setup_inputs(seed: int = 0) -> dict:
    arg_keys = jax.random.split(jax.random.key(seed), 8)
    return {
        "amplitudes": normal_values(arg_keys[0], (NI, O, V, V), 1.0, 6.0, ((0, 32), (1, 16)), jnp.float32),
        "driver": normal_values(arg_keys[1], (NI, O, V, V), 3.0, 15.0, ((0, 32), (1, 16)), jnp.float32),
        "fit_vectors": normal_values(arg_keys[2], (O, NQ, V), (O * V // 4) ** -0.5, 0.09375, ((0, 16), (1, 32)), jnp.float32),
        "ladder_factors": normal_values(arg_keys[3], (NL, V, V), (2 * V) ** -0.5, 0.25, ((1, 32),), jnp.float32),
        "row_energy": jnp.clip(-2.0 + 1.7 * jax.random.uniform(arg_keys[4], (NI,), jnp.float32) ** block_levels(arg_keys[4], (NI,), ((0, 32),), -0.2, 0.2), -2.0, -0.3),
        "occupied_energy": jnp.clip(-2.0 + 1.7 * jax.random.uniform(arg_keys[5], (O,), jnp.float32) ** block_levels(arg_keys[5], (O,), ((0, 16),), -0.2, 0.2), -2.0, -0.3),
        "virtual_energy": jnp.clip(jax.random.uniform(arg_keys[6], (V,), jnp.float32, 0.5, 3.0), 0.5, 3.0),
    }


def reference(amplitudes, driver, fit_vectors, ladder_factors, row_energy, occupied_energy, virtual_energy):
    highest = lax.Precision.HIGHEST
    pair_energy = virtual_energy[:, None] + virtual_energy[None, :]

    def update_row(operands):
        row_amps, row_driver, energy = operands
        denominator = pair_energy[None, :, :] - energy - occupied_energy[:, None, None]
        for iteration in range(ITERS):
            fitted = jnp.einsum("kac,kqc->aq", row_amps, fit_vectors, precision=highest)
            cycle_term = jnp.einsum("aq,jqb->jab", fitted, fit_vectors, precision=highest)
            ladder_term = jnp.zeros_like(row_amps)
            for factor_index in range(NL):
                factor = ladder_factors[factor_index]
                left_side = jnp.einsum("ac,jcd->jad", factor, row_amps, precision=highest)
                ladder_term = ladder_term + jnp.einsum("jad,bd->jab", left_side, factor, precision=highest)
            row_amps = (row_driver + cycle_term + ladder_term) / denominator
        return row_amps

    return lax.map(update_row, (amplitudes, driver, row_energy))
```

```python
import jax
import jax.numpy as jnp
from jax import lax
from jax.sharding import Mesh
from jax.sharding import PartitionSpec as P

ITERS = 2
HIGH = lax.Precision.HIGH
AXES = ("y_lo", "z", "y_hi", "x", "core")
WIDE = ("y_lo", "z")
NARROW = ("y_hi", "x", "core")


def shifted(n, step):
    return [(i, (i + step) % n) for i in range(n)]


def along_z(shard, step):
    pairs = []
    for z in range(8):
        for core in range(2):
            to = (z + step) % 8 if core == 0 else (z - step) % 8
            pairs.append((2 * z + core, 2 * to + core))
    return lax.ppermute(shard, ("z", "core"), pairs)


def ring_gather(block):
    half = block.shape[1] // 2
    up, down = [block], [block]
    for _ in range(3):
        up.append(along_z(up[-1], 1))
        down.append(along_z(down[-1], -1))
    far = jnp.concatenate(
        [along_z(up[-1][:, :half], 1), along_z(down[-1][:, half:], -1)], axis=1
    )
    return up[0], up[1:], down[1:], far


def summed(own, far, up, down):
    first = lax.axis_index("core") == 0
    keep = jnp.stack([jnp.where(first, own, far)] + up)
    send = jnp.stack([jnp.where(first, far, own)] + down)
    keep = keep + lax.ppermute(send, "core", [(0, 1), (1, 0)])
    piece = lax.all_to_all(keep, "x", 0, 0, tiled=True).sum(axis=0)
    piece = piece + lax.ppermute(piece, "y_hi", [(0, 1), (1, 0)])
    kept = lax.all_gather(piece, "x")
    other = lax.ppermute(kept, "core", [(0, 1), (1, 0)])
    own = jnp.where(first, kept[0], other[0])
    far = jnp.where(first, other[0], kept[0])
    return own, far, [kept[n] for n in (1, 2, 3)], [other[n] for n in (1, 2, 3)]


def fitted_piece(current, fit):
    return jnp.einsum("kac,kqc->aq", current, fit, precision=HIGH)


def local(
    amplitudes, driver, fit_vectors, ladder_factors, row_energy, occupied_energy, virtual_energy
):
    current, driver = amplitudes[0], driver[0]
    pair_energy = virtual_energy[:, None] + virtual_energy[None, :]
    denominator = pair_energy[None] - row_energy[0] - occupied_energy[:, None, None]

    rows = ladder_factors.reshape(16, 256)
    mine = jnp.concatenate([fit_vectors.reshape(128, 256), rows])
    columns = [mine] + [lax.ppermute(mine, "y_lo", shifted(4, s)) for s in (3, 2, 1)]
    fit_part = jnp.concatenate([c[:128].reshape(4, 32, 256) for c in columns], axis=1)
    ladder_part = jnp.stack([c[128:] for c in columns])
    block = jnp.concatenate([fit_part, ladder_part], axis=1)
    own, up, down, far = ring_gather(block)

    first = lax.axis_index("core") == 0
    ahead = [jnp.where(first, d[:, 128:], u[:, 128:]) for u, d in zip(up, down)]
    behind = [jnp.where(first, u[:, 128:], d[:, 128:]) for u, d in zip(up, down)]
    turn = jnp.stack([own[:, 128:]] + ahead + [far[:, 128:]] + behind[::-1], axis=1)
    turn = jnp.roll(turn, (lax.axis_index("y_lo"), lax.axis_index("z")), axis=(0, 1))
    ladder = turn.reshape(32, 2, 8, 256).transpose(1, 0, 2, 3).reshape(2, 256, 256)

    parts = [own, far] + up + down
    fits = [p[:, :128] for p in parts]
    whole_fit = jnp.concatenate(fits, axis=1)
    pieces = [fitted_piece(current, f) for f in fits]
    for iteration in range(ITERS):
        if iteration:
            whole = fitted_piece(current, whole_fit)
            pieces = [whole[:, 128 * n : 128 * (n + 1)] for n in range(8)]
        s_own, s_far, s_up, s_down = summed(pieces[0], pieces[1], pieces[2:5], pieces[5:8])
        fitted = jnp.concatenate([s_own, s_far] + s_up + s_down, axis=1)
        ladder_term = jnp.zeros_like(current)
        for p in range(2):
            left = jnp.einsum("ac,jcd->jad", ladder[p], current, precision=HIGH)
            ladder_term = ladder_term + jnp.einsum("jad,bd->jab", left, ladder[p], precision=HIGH)
        cycle = jnp.einsum("aq,jqb->jab", fitted, whole_fit, precision=HIGH)
        current = (driver + cycle + ladder_term) / denominator
    return current[None]


def solution(mesh):
    torus = Mesh(mesh.devices.reshape(4, 8, 2, 4, 2), AXES)
    in_specs = (
        P(WIDE, NARROW, None, None),
        P(WIDE, NARROW, None, None),
        P(NARROW, WIDE, None),
        P(None, WIDE, None),
        P(WIDE),
        P(NARROW),
        P(),
    )
    out_specs = P(WIDE, NARROW, None, None)
    return jax.shard_map(local, mesh=torus, in_specs=in_specs, out_specs=out_specs, check_vma=False)
```

```python
import jax
import jax.numpy as jnp
from jax import lax
from jax.experimental import pallas as pl
from jax.experimental.pallas import tpu as pltpu
from jax.sharding import Mesh
from jax.sharding import PartitionSpec as P

ITERS = 2
AXES = ("y_lo", "z", "y_hi", "x", "core")
WIDE = ("y_lo", "z")
NARROW = ("y_hi", "x", "core")
F32, BF16 = jnp.float32, jnp.bfloat16
VMEM = pl.BlockSpec(memory_space=pltpu.VMEM)
SMEM = pl.BlockSpec(memory_space=pltpu.SMEM)
ROWS = 136
NT = (((1,), (1,)), ((), ()))
NN = (((1,), (0,)), ((), ()))


def call(kernel, name, outs, in_specs, *operands):
    return pl.pallas_call(
        kernel,
        name=name,
        out_shape=[jax.ShapeDtypeStruct(s, d) for s, d in outs],
        in_specs=in_specs,
        out_specs=[VMEM] * len(outs),
        compiler_params=pltpu.CompilerParams(vmem_limit_bytes=8 << 20),
    )(*operands)


def split(value):
    high = value.astype(BF16)
    return high, (value - high.astype(F32)).astype(BF16)


def joined(pieces, axis):
    return pieces[0] if len(pieces) == 1 else jnp.concatenate(pieces, axis=axis)


def dot3(a, b, dims):
    (a0, a1), (b0, b1) = a, b
    left = joined([a0, a0, a1], 1)
    right = joined([b0, b1, b0], 1 if dims == NT else 0)
    return lax.dot_general(left, right, dims, preferred_element_type=F32)


def own_kernel(place, fit, factors, out):
    for k in range(4):
        out[32 * k : 32 * (k + 1)] = fit[k]
    out[128:] = jnp.where(place[2] == 0, factors[0], factors[1])


def add_kernel(one, two, out):
    out[...] = one[...] + two[: one.shape[0]]


def total_kernel(parts, out):
    out[...] = (parts[0] + parts[1]) + (parts[2] + parts[3])


def copies_kernel(one, two, out):
    total = one[...] + two[...]
    for n in range(4):
        out[n] = total


def pack_kernel(*refs):
    *columns, block = refs
    for s, column in enumerate(columns):
        for k in range(4):
            block[k, 32 * s : 32 * (s + 1)] = column[32 * k : 32 * (k + 1)]
        block[s, 128:] = column[128:]


def halves_kernel(amps, high, low):
    for k in range(4):
        high[k], low[k] = split(amps[k])


def fit_chunk(amps, chunk, high, low):
    for k in range(4):
        high[k], low[k] = split(chunk[k])
    a = tuple(joined([ref[k] for k in range(4)], 1) for ref in amps)
    b = tuple(joined([ref[k] for k in range(4)], 1) for ref in (high, low))
    return dot3(a, b, NT)


def fit_kernel(n, *refs):
    chunks, amps, outs = refs[:n], refs[n : n + 2], refs[n + 2 :]
    for chunk, piece, high, low in zip(chunks, outs[:n], outs[n : 2 * n], outs[2 * n :]):
        piece[...] = fit_chunk(amps, [chunk[k, :128] for k in range(4)], high, low)


def last_kernel(place, *refs):
    far_a, far_b, *refs = refs
    chunks, pieces, amps = refs[:7], refs[7:14], refs[14:16]
    keep, send, high, low, ladder = refs[16:]
    half = far_a.shape[1]
    values = [jnp.concatenate([far_a[k], far_b[k, : 128 - half]], axis=0) for k in range(4)]
    far = fit_chunk(amps, values, high, low)
    own = pieces[0][...]
    first = place[2] == 0
    keep[0] = jnp.where(first, own, far)
    send[0] = jnp.where(first, far, own)
    for n in range(3):
        below, above = pieces[1 + n][...], pieces[4 + n][...]
        keep[1 + n] = jnp.where(first, below, above)
        send[1 + n] = jnp.where(first, above, below)
    for n, step in enumerate((0, -1, -2, -3, 1, 2, 3, 4)):
        z = lax.rem(place[1] + 8 + step, 8)
        for s in range(4):
            y = lax.rem(place[0] + s, 4)
            rows = chunks[n][s, 128:] if n < 7 else far_b[s, 128 - half :]
            ladder[pl.ds(pl.multiple_of((8 * y + z) * 8, 8), 8)] = rows
    send[4] = ladder[:, :128]
    send[5] = ladder[:, 128:]


def ladder_kernel(n, start, amps, own, other, out):
    factors = [split(jnp.concatenate([ref[n], ref[n + 1]], axis=1)) for ref in (own, other)]
    stack = tuple(joined([f[i] for f in factors], 0) for i in range(2))
    wide = tuple(joined([f[i] for f in factors], 1) for i in range(2))
    for j in range(4):
        left = dot3(stack, split(amps[j]), NN)
        left = split(jnp.concatenate([left[:256], left[256:]], axis=1))
        out[j] = start[j] + dot3(left, wide, NT)


def step_kernel(last, place, row, occupied, pair, kept, other, start, *refs):
    highs, lows = refs[:8], refs[8:16]
    current, *outs = refs[16:]
    first = place[2] == 0
    order = [jnp.where(first, kept[n], other[n]) for n in range(4)]
    order += [jnp.where(first, other[n], kept[n]) for n in (1, 2, 3, 0)]
    fitted = split(jnp.concatenate(order, axis=1))
    for j in range(4):
        fit = tuple(joined([ref[j] for ref in group], 0) for group in (highs, lows))
        cycle = dot3(fitted, fit, NN)
        below = pair[...] - row[0] - occupied[j]
        current[j] = (start[j] + cycle) / below
    if last:
        return
    keep, send = outs
    amps = [split(current[k]) for k in range(4)]
    amps = tuple(joined([a[i] for a in amps], 1) for i in range(2))
    for n, (one, two) in enumerate(((0, 7), (1, 4), (2, 5), (3, 6))):
        fit = []
        for group in (highs, lows):
            pair_of = [joined([group[m][k] for k in range(4)], 1) for m in (one, two)]
            fit.append(jnp.concatenate(pair_of, axis=0))
        piece = dot3(amps, fit, NT)
        keep[n] = jnp.where(first, piece[:, :128], piece[:, 128:])
        send[n] = jnp.where(first, piece[:, 128:], piece[:, :128])


def shifted(n, step):
    return [(i, (i + step) % n) for i in range(n)]


def along_z(shard, step):
    return lax.ppermute(shard, "z", shifted(8, step))


def swapped(shard, axis):
    return lax.ppermute(shard, axis, [(0, 1), (1, 0)])


def added(one, two):
    return call(add_kernel, "add", [(one.shape, F32)], [VMEM] * 2, one, two)[0]


def summed(half):
    arrived = lax.all_to_all(half, "x", 0, 0, tiled=True)
    (piece,) = call(total_kernel, "total", [(half.shape[1:], F32)], [VMEM], arrived)
    other = swapped(piece, "y_hi")
    (copies,) = call(copies_kernel, "copies", [(half.shape, F32)], [VMEM] * 2, piece, other)
    kept = lax.all_to_all(copies, "x", 0, 0, tiled=True)
    return kept, swapped(kept, "core")


def local(
    amplitudes, driver, fit_vectors, ladder_factors, row_energy, occupied_energy, virtual_energy
):
    amps, driver = amplitudes[0], driver[0]
    core = lax.axis_index("core")
    place = jnp.stack([lax.axis_index("y_lo"), lax.axis_index("z"), core]).astype(jnp.int32)
    pair = virtual_energy[:, None] + virtual_energy[None, :]
    (mine,) = call(
        own_kernel,
        "own",
        [((ROWS, 256), F32)],
        [SMEM] + [VMEM] * 2,
        place, fit_vectors, ladder_factors,
    )
    columns = [mine] + [lax.ppermute(mine, "y_lo", shifted(4, s)) for s in (3, 2, 1)]
    whole, pieced = ((4, 256, 256), BF16), ((4, 128, 256), BF16)
    (block,) = call(pack_kernel, "pack", [((4, ROWS, 256), F32)], [VMEM] * 4, *columns)
    t = call(halves_kernel, "halves", [whole, whole], [VMEM], amps)

    def fits(name, *chunks):
        n = len(chunks)
        outs = [((256, 128), F32)] * n + [pieced] * (2 * n)
        got = call(
            lambda *refs: fit_kernel(n, *refs), name, outs, [VMEM] * (n + 2), *chunks, *t
        )
        return got[:n], got[n : 2 * n], got[2 * n :]

    up, down, found = [block], [block], [fits("fit_own", block)]
    for n in range(3):
        up.append(along_z(up[-1], 1))
        down.append(along_z(down[-1], -1))
        found.append(fits("fit", up[-1], down[-1]))
    far = [along_z(up[-1][:, :64], 1), along_z(down[-1][:, 64:], -1)]
    pieces, highs, lows = (
        [found[0][i][0]] + [f[i][0] for f in found[1:]] + [f[i][1] for f in found[1:]]
        for i in range(3)
    )
    keep, send, high, low, _ = call(
        last_kernel,
        "fit_last",
        [((4, 256, 128), F32), ((6, 256, 128), F32), pieced, pieced, ((256, 256), F32)],
        [SMEM] + [VMEM] * 18,
        place, *far, *up, *down[1:], *pieces, *t,
    )
    highs, lows = highs + [high], lows + [low]
    got = swapped(send, "core")
    kept = added(keep, got)
    ladder_own, ladder_other = send, got
    for iteration in range(ITERS):
        last = iteration == ITERS - 1
        (start,) = call(
            lambda *refs: ladder_kernel(4, *refs),
            "ladder",
            [((4, 256, 256), F32)],
            [VMEM] * 4,
            driver, amps, ladder_own, ladder_other,
        )
        kept, other = summed(kept)
        outs = [((4, 256, 256), F32)] + ([] if last else [((4, 256, 128), F32)] * 2)
        amps, *rest = call(
            lambda *refs: step_kernel(last, *refs),
            "step",
            outs,
            [SMEM] * 3 + [VMEM] * 20,
            place, row_energy, occupied_energy, pair, kept, other, start, *highs, *lows,
        )
        if not last:
            kept = added(rest[0], swapped(rest[1], "core"))
    return amps[None]


def solution(mesh):
    torus = Mesh(mesh.devices.reshape(4, 8, 2, 4, 2), AXES)
    in_specs = (
        P(WIDE, NARROW, None, None),
        P(WIDE, NARROW, None, None),
        P(NARROW, WIDE, None),
        P(None, WIDE, None),
        P(WIDE),
        P(NARROW),
        P(),
    )
    out_specs = P(WIDE, NARROW, None, None)
    return jax.shard_map(local, mesh=torus, in_specs=in_specs, out_specs=out_specs, check_vma=False)
```

```python
import jax
import jax.numpy as jnp
from jax import lax
from jax.experimental import pallas as pl
from jax.experimental.pallas import tpu as pltpu
from jax.sharding import Mesh
from jax.sharding import PartitionSpec as P

ITERS = 2
AXES = ("y_lo", "z", "y_hi", "x", "core")
WIDE = ("y_lo", "z")
NARROW = ("y_hi", "x", "core")
F32, BF16 = jnp.float32, jnp.bfloat16
VMEM = pl.BlockSpec(memory_space=pltpu.VMEM)
SMEM = pl.BlockSpec(memory_space=pltpu.SMEM)
ROWS = 136
PAIR = 272
NT = (((1,), (1,)), ((), ()))
NN = (((1,), (0,)), ((), ()))


def call(kernel, name, outs, in_specs, *operands):
    return pl.pallas_call(
        kernel,
        name=name,
        out_shape=[jax.ShapeDtypeStruct(s, d) for s, d in outs],
        in_specs=in_specs,
        out_specs=[VMEM] * len(outs),
        compiler_params=pltpu.CompilerParams(vmem_limit_bytes=8 << 20),
    )(*operands)


def split(value):
    high = value.astype(BF16)
    return high, (value - high.astype(F32)).astype(BF16)


def joined(pieces, axis):
    return pieces[0] if len(pieces) == 1 else jnp.concatenate(pieces, axis=axis)


def dot3(a, b, dims):
    (a0, a1), (b0, b1) = a, b
    left = joined([a0, a0, a1], 1)
    right = joined([b0, b1, b0], 1 if dims == NT else 0)
    return lax.dot_general(left, right, dims, preferred_element_type=F32)


def own_kernel(place, fit, factors, out):
    for k in range(4):
        out[32 * k : 32 * (k + 1)] = fit[k]
    out[128:] = jnp.where(place[2] == 0, factors[0], factors[1])


def add_kernel(one, two, out):
    out[...] = one[...] + two[: one.shape[0]]


def total_kernel(parts, out):
    out[...] = (parts[0] + parts[1]) + (parts[2] + parts[3])


def copies_kernel(one, two, out):
    total = one[...] + two[...]
    for n in range(4):
        out[n] = total


def pack_kernel(one, two, out):
    for c, column in enumerate((one, two)):
        for k in range(4):
            at = 64 * k + 32 * c
            out[at : at + 32] = column[32 * k : 32 * (k + 1)]
        out[256 + 8 * c : 264 + 8 * c] = column[128:]


def halves_kernel(amps, high, low):
    for k in range(4):
        high[k], low[k] = split(amps[k])


def fit_chunk(amps, near, beyond, high, low):
    for k in range(4):
        at = slice(64 * k, 64 * (k + 1))
        high[k], low[k] = split(jnp.concatenate([near[at], beyond[at]], axis=0))
    a = tuple(joined([ref[k] for k in range(4)], 1) for ref in amps)
    b = tuple(joined([ref[k] for k in range(4)], 1) for ref in (high, low))
    return dot3(a, b, NT)


def fit_kernel(n, *refs):
    chunks, amps, outs = refs[: 2 * n], refs[2 * n : 2 * n + 2], refs[2 * n + 2 :]
    for c in range(n):
        outs[c][...] = fit_chunk(
            amps, chunks[2 * c], chunks[2 * c + 1], outs[n + c], outs[2 * n + c]
        )


def last_kernel(place, *refs):
    chunks, pieces, amps = refs[:16], refs[16:23], refs[23:25]
    keep, send, high, low, ladder = refs[25:]
    far = fit_chunk(amps, chunks[14], chunks[15], high, low)
    own = pieces[0][...]
    first = place[2] == 0
    keep[0] = jnp.where(first, own, far)
    send[0] = jnp.where(first, far, own)
    for n in range(3):
        below, above = pieces[1 + n][...], pieces[4 + n][...]
        keep[1 + n] = jnp.where(first, below, above)
        send[1 + n] = jnp.where(first, above, below)
    for n, step in enumerate((0, -1, -2, -3, 1, 2, 3, 4)):
        z = lax.rem(place[1] + 8 + step, 8)
        for s in range(4):
            y = lax.rem(place[0] + s, 4)
            at = 256 + 8 * (s % 2)
            rows = chunks[2 * n + s // 2][at : at + 8]
            ladder[pl.ds(pl.multiple_of((8 * y + z) * 8, 8), 8)] = rows
    send[4] = ladder[:, :128]
    send[5] = ladder[:, 128:]


def ladder_kernel(n, start, amps, own, other, out):
    factors = [split(jnp.concatenate([ref[n], ref[n + 1]], axis=1)) for ref in (own, other)]
    stack = tuple(joined([f[i] for f in factors], 0) for i in range(2))
    wide = tuple(joined([f[i] for f in factors], 1) for i in range(2))
    for j in range(4):
        left = dot3(stack, split(amps[j]), NN)
        left = split(jnp.concatenate([left[:256], left[256:]], axis=1))
        out[j] = start[j] + dot3(left, wide, NT)


def step_kernel(last, place, row, occupied, pair, kept, other, start, *refs):
    highs, lows = refs[:8], refs[8:16]
    current, *outs = refs[16:]
    first = place[2] == 0
    order = [jnp.where(first, kept[n], other[n]) for n in range(4)]
    order += [jnp.where(first, other[n], kept[n]) for n in (1, 2, 3, 0)]
    fitted = split(jnp.concatenate(order, axis=1))
    for j in range(4):
        fit = tuple(joined([ref[j] for ref in group], 0) for group in (highs, lows))
        cycle = dot3(fitted, fit, NN)
        below = pair[...] - row[0] - occupied[j]
        current[j] = (start[j] + cycle) / below
    if last:
        return
    keep, send = outs
    amps = [split(current[k]) for k in range(4)]
    amps = tuple(joined([a[i] for a in amps], 1) for i in range(2))
    for n, (one, two) in enumerate(((0, 7), (1, 4), (2, 5), (3, 6))):
        fit = []
        for group in (highs, lows):
            pair_of = [joined([group[m][k] for k in range(4)], 1) for m in (one, two)]
            fit.append(jnp.concatenate(pair_of, axis=0))
        piece = dot3(amps, fit, NT)
        keep[n] = jnp.where(first, piece[:, :128], piece[:, 128:])
        send[n] = jnp.where(first, piece[:, 128:], piece[:, :128])


def shifted(n, step):
    return [(i, (i + step) % n) for i in range(n)]


def along_z(shard, step):
    return lax.ppermute(shard, "z", shifted(8, step))


def swapped(shard, axis):
    return lax.ppermute(shard, axis, [(0, 1), (1, 0)])


def added(one, two):
    return call(add_kernel, "add", [(one.shape, F32)], [VMEM] * 2, one, two)[0]


def summed(half):
    arrived = lax.all_to_all(half, "x", 0, 0, tiled=True)
    (piece,) = call(total_kernel, "total", [(half.shape[1:], F32)], [VMEM], arrived)
    other = swapped(piece, "y_hi")
    (copies,) = call(copies_kernel, "copies", [(half.shape, F32)], [VMEM] * 2, piece, other)
    kept = lax.all_to_all(copies, "x", 0, 0, tiled=True)
    return kept, swapped(kept, "core")


def local(
    amplitudes, driver, fit_vectors, ladder_factors, row_energy, occupied_energy, virtual_energy
):
    amps, driver = amplitudes[0], driver[0]
    core = lax.axis_index("core")
    place = jnp.stack([lax.axis_index("y_lo"), lax.axis_index("z"), core]).astype(jnp.int32)
    pair = virtual_energy[:, None] + virtual_energy[None, :]
    (mine,) = call(
        own_kernel,
        "own",
        [((ROWS, 256), F32)],
        [SMEM] + [VMEM] * 2,
        place, fit_vectors, ladder_factors,
    )
    columns = [mine] + [lax.ppermute(mine, "y_lo", shifted(4, s)) for s in (3, 2, 1)]
    whole, pieced = ((4, 256, 256), BF16), ((4, 128, 256), BF16)
    near, beyond = (
        call(pack_kernel, "pack", [((PAIR, 256), F32)], [VMEM] * 2, *columns[n : n + 2])[0]
        for n in (0, 2)
    )
    t = call(halves_kernel, "halves", [whole, whole], [VMEM], amps)

    def fits(name, *chunks):
        n = len(chunks)
        outs = [((256, 128), F32)] * n + [pieced] * (2 * n)
        flat = [half for chunk in chunks for half in chunk]
        got = call(
            lambda *refs: fit_kernel(n, *refs), name, outs, [VMEM] * (2 * n + 2), *flat, *t
        )
        return got[:n], got[n : 2 * n], got[2 * n :]

    up, down, found = [(near, beyond)], [(near, beyond)], [fits("fit_own", (near, beyond))]
    for n in range(3):
        rising, falling = [], []
        for half in range(2):
            rising.append(along_z(up[-1][half], 1))
            falling.append(along_z(down[-1][half], -1))
        up.append(rising)
        down.append(falling)
        found.append(fits("fit", up[-1], down[-1]))
    far = [along_z(up[-1][0], 1), along_z(down[-1][1], -1)]
    pieces, highs, lows = (
        [found[0][i][0]] + [f[i][0] for f in found[1:]] + [f[i][1] for f in found[1:]]
        for i in range(3)
    )
    chunks = [half for chunk in up + down[1:] + [far] for half in chunk]
    keep, send, high, low, _ = call(
        last_kernel,
        "fit_last",
        [((4, 256, 128), F32), ((6, 256, 128), F32), pieced, pieced, ((256, 256), F32)],
        [SMEM] + [VMEM] * 25,
        place, *chunks, *pieces, *t,
    )
    highs, lows = highs + [high], lows + [low]
    got = swapped(send, "core")
    kept = added(keep, got)
    ladder_own, ladder_other = send, got
    for iteration in range(ITERS):
        last = iteration == ITERS - 1
        (start,) = call(
            lambda *refs: ladder_kernel(4, *refs),
            "ladder",
            [((4, 256, 256), F32)],
            [VMEM] * 4,
            driver, amps, ladder_own, ladder_other,
        )
        kept, other = summed(kept)
        outs = [((4, 256, 256), F32)] + ([] if last else [((4, 256, 128), F32)] * 2)
        amps, *rest = call(
            lambda *refs: step_kernel(last, *refs),
            "step",
            outs,
            [SMEM] * 3 + [VMEM] * 20,
            place, row_energy, occupied_energy, pair, kept, other, start, *highs, *lows,
        )
        if not last:
            kept = added(rest[0], swapped(rest[1], "core"))
    return amps[None]


def solution(mesh):
    torus = Mesh(mesh.devices.reshape(4, 8, 2, 4, 2), AXES)
    in_specs = (
        P(WIDE, NARROW, None, None),
        P(WIDE, NARROW, None, None),
        P(NARROW, WIDE, None),
        P(None, WIDE, None),
        P(WIDE),
        P(NARROW),
        P(),
    )
    out_specs = P(WIDE, NARROW, None, None)
    return jax.shard_map(local, mesh=torus, in_specs=in_specs, out_specs=out_specs, check_vma=False)
```

```python
import jax
import jax.numpy as jnp
from jax import lax
from jax.experimental import pallas as pl
from jax.experimental.pallas import tpu as pltpu
from jax.sharding import Mesh
from jax.sharding import PartitionSpec as P

ITERS = 2
AXES = ("y_lo", "z", "y_hi", "x", "core")
WIDE = ("y_lo", "z")
NARROW = ("y_hi", "x", "core")
F32, BF16 = jnp.float32, jnp.bfloat16
VMEM = pl.BlockSpec(memory_space=pltpu.VMEM)
SMEM = pl.BlockSpec(memory_space=pltpu.SMEM)
ROWS = 136
PAIR = 272
ORDER = (0, 1, 2, 3, 7, 4, 5, 6)
NT = (((1,), (1,)), ((), ()))
NN = (((1,), (0,)), ((), ()))


def call(kernel, name, outs, in_specs, *operands):
    return pl.pallas_call(
        kernel,
        name=name,
        out_shape=[jax.ShapeDtypeStruct(s, d) for s, d in outs],
        in_specs=in_specs,
        out_specs=[VMEM] * len(outs),
        compiler_params=pltpu.CompilerParams(vmem_limit_bytes=8 << 20),
    )(*operands)


def split(value):
    high = value.astype(BF16)
    return high, (value - high.astype(F32)).astype(BF16)


def joined(pieces, axis):
    return pieces[0] if len(pieces) == 1 else jnp.concatenate(pieces, axis=axis)


def dot3(a, b, dims):
    (a0, a1), (b0, b1) = a, b
    left = joined([a0, a0, a1], 1)
    right = joined([b0, b1, b0], 1 if dims == NT else 0)
    return lax.dot_general(left, right, dims, preferred_element_type=F32)


def own_kernel(place, fit, factors, out):
    for k in range(4):
        out[32 * k : 32 * (k + 1)] = fit[k]
    out[128:] = jnp.where(place[2] == 0, factors[0], factors[1])


def add_kernel(one, two, out):
    out[...] = one[...] + two[: one.shape[0]]


def total_kernel(parts, out):
    out[...] = (parts[0] + parts[1]) + (parts[2] + parts[3])


def copies_kernel(one, two, _, out):
    total = one[...] + two[...]
    for n in range(4):
        out[n] = total


def pack_kernel(one, two, out):
    for c, column in enumerate((one, two)):
        for k in range(4):
            at = 64 * k + 32 * c
            out[at : at + 32] = column[32 * k : 32 * (k + 1)]
        out[256 + 8 * c : 264 + 8 * c] = column[128:]


def early_kernel(row, occupied, amps, virtual, high, low, below):
    across = jnp.broadcast_to(virtual[...], (256, 256))
    pair = jnp.transpose(across) + across
    for k in range(4):
        high[k], low[k] = split(amps[k])
        below[k] = pair - row[0] - occupied[k]


def fit_chunk(amps, near, beyond, high, low):
    for k in range(4):
        at = slice(64 * k, 64 * (k + 1))
        high[k], low[k] = split(jnp.concatenate([near[at], beyond[at]], axis=0))
    a = tuple(joined([ref[k] for k in range(4)], 1) for ref in amps)
    b = tuple(joined([ref[k] for k in range(4)], 1) for ref in (high, low))
    return dot3(a, b, NT)


def fit_kernel(n, *refs):
    chunks, amps, outs = refs[: 2 * n], refs[2 * n : 2 * n + 2], refs[2 * n + 2 :]
    for c in range(n):
        outs[c][...] = fit_chunk(
            amps, chunks[2 * c], chunks[2 * c + 1], outs[n + c], outs[2 * n + c]
        )


def last_kernel(place, *refs):
    chunks, pieces, amps = refs[:16], refs[16:23], refs[23:25]
    keep, send, high, low, ladder = refs[25:]
    far = fit_chunk(amps, chunks[14], chunks[15], high, low)
    own = pieces[0][...]
    first = place[2] == 0
    keep[0] = jnp.where(first, own, far)
    send[0] = jnp.where(first, far, own)
    for n in range(3):
        below, above = pieces[1 + n][...], pieces[4 + n][...]
        keep[1 + n] = jnp.where(first, below, above)
        send[1 + n] = jnp.where(first, above, below)
    for n, step in enumerate((0, -1, -2, -3, 1, 2, 3, 4)):
        z = lax.rem(place[1] + 8 + step, 8)
        for s in range(4):
            y = lax.rem(place[0] + s, 4)
            at = 256 + 8 * (s % 2)
            rows = chunks[2 * n + s // 2][at : at + 8]
            ladder[pl.ds(pl.multiple_of((8 * y + z) * 8, 8), 8)] = rows
    send[4] = ladder[:, :128]
    send[5] = ladder[:, 128:]


def ladder_kernel(n, start, amps, own, other, out):
    factors = [split(jnp.concatenate([ref[n], ref[n + 1]], axis=1)) for ref in (own, other)]
    stack = tuple(joined([f[i] for f in factors], 0) for i in range(2))
    wide = tuple(joined([f[i] for f in factors], 1) for i in range(2))
    for j in range(4):
        left = dot3(stack, split(amps[j]), NN)
        left = split(jnp.concatenate([left[:256], left[256:]], axis=1))
        out[j] = start[j] + dot3(left, wide, NT)


def by_core(place, body):
    @pl.when(place[2] == 0)
    def _():
        body(ORDER)

    @pl.when(place[2] != 0)
    def _():
        body(ORDER[4:] + ORDER[:4])


def cycle_half(pieces, highs, lows, chosen, j):
    fit = tuple(joined([group[m][j] for m in chosen], 0) for group in (highs, lows))
    return dot3(pieces, fit, NN)


def fitted_half(amps, highs, lows, chosen, out):
    for n in (0, 2):
        fit = []
        for group in (highs, lows):
            two = [joined([group[m][k] for k in range(4)], 1) for m in chosen[n : n + 2]]
            fit.append(jnp.concatenate(two, axis=0))
        piece = dot3(amps, fit, NT)
        out[n], out[n + 1] = piece[:, :128], piece[:, 128:]


def side_by_side(ref):
    return jnp.concatenate([ref[n] for n in range(4)], axis=1)


def kept_kernel(place, kept, start, *refs):
    highs, lows, out = refs[:8], refs[8:16], refs[16]

    def body(order):
        pieces = split(side_by_side(kept))
        for j in range(4):
            out[j] = start[j] + cycle_half(pieces, highs, lows, order[:4], j)

    by_core(place, body)


def step_kernel(last, place, below, other, start, *refs):
    highs, lows = refs[:8], refs[8:16]
    current, *outs = refs[16:]

    def body(order):
        pieces = split(side_by_side(other))
        for j in range(4):
            cycle = cycle_half(pieces, highs, lows, order[4:], j)
            current[j] = (start[j] + cycle) / below[j]
        if last:
            return
        send, high, low = outs
        for k in range(4):
            high[k], low[k] = split(current[k])
        amps = tuple(joined([ref[k] for k in range(4)], 1) for ref in (high, low))
        fitted_half(amps, highs, lows, order[4:], send)

    by_core(place, body)


def keep_kernel(place, high, low, *refs):
    highs, lows, keep = refs[:8], refs[8:16], refs[16]

    def body(order):
        amps = tuple(joined([ref[k] for k in range(4)], 1) for ref in (high, low))
        fitted_half(amps, highs, lows, order[:4], keep)

    by_core(place, body)


def shifted(n, step):
    return [(i, (i + step) % n) for i in range(n)]


def along_z(shard, step):
    return lax.ppermute(shard, "z", shifted(8, step))


def swapped(shard, axis):
    return lax.ppermute(shard, axis, [(0, 1), (1, 0)])


def added(one, two):
    return call(add_kernel, "add", [(one.shape, F32)], [VMEM] * 2, one, two)[0]


def summed(half, first):
    arrived = lax.all_to_all(half, "x", 0, 0, tiled=True)
    (piece,) = call(total_kernel, "total", [(half.shape[1:], F32)], [VMEM], arrived)
    other = swapped(piece, "y_hi")
    (copies,) = call(copies_kernel, "copies", [(half.shape, F32)], [VMEM] * 3, piece, other, first)
    kept = lax.all_to_all(copies, "x", 0, 0, tiled=True)
    return kept, swapped(kept, "core")


def local(
    amplitudes, driver, fit_vectors, ladder_factors, row_energy, occupied_energy, virtual_energy
):
    amps, driver = amplitudes[0], driver[0]
    core = lax.axis_index("core")
    place = jnp.stack([lax.axis_index("y_lo"), lax.axis_index("z"), core]).astype(jnp.int32)
    (mine,) = call(
        own_kernel,
        "own",
        [((ROWS, 256), F32)],
        [SMEM] + [VMEM] * 2,
        place, fit_vectors, ladder_factors,
    )
    columns = [mine] + [lax.ppermute(mine, "y_lo", shifted(4, s)) for s in (3, 2, 1)]
    whole, pieced = ((4, 256, 256), BF16), ((4, 128, 256), BF16)
    near, beyond = (
        call(pack_kernel, "pack", [((PAIR, 256), F32)], [VMEM] * 2, *columns[n : n + 2])[0]
        for n in (0, 2)
    )
    *t, below = call(
        early_kernel,
        "early",
        [whole, whole, ((4, 256, 256), F32)],
        [SMEM] * 2 + [VMEM] * 2,
        row_energy, occupied_energy, amps, virtual_energy.reshape(1, 256),
    )

    def fits(name, *chunks):
        n = len(chunks)
        outs = [((256, 128), F32)] * n + [pieced] * (2 * n)
        flat = [half for chunk in chunks for half in chunk]
        got = call(
            lambda *refs: fit_kernel(n, *refs), name, outs, [VMEM] * (2 * n + 2), *flat, *t
        )
        return got[:n], got[n : 2 * n], got[2 * n :]

    up, down, found = [(near, beyond)], [(near, beyond)], [fits("fit_own", (near, beyond))]
    for n in range(3):
        rising, falling = [], []
        for half in range(2):
            rising.append(along_z(up[-1][half], 1))
            falling.append(along_z(down[-1][half], -1))
        up.append(rising)
        down.append(falling)
        found.append(fits("fit", up[-1], down[-1]))
    far = [along_z(up[-1][0], 1), along_z(down[-1][1], -1)]
    pieces, highs, lows = (
        [found[0][i][0]] + [f[i][0] for f in found[1:]] + [f[i][1] for f in found[1:]]
        for i in range(3)
    )
    chunks = [half for chunk in up + down[1:] + [far] for half in chunk]
    keep, send, high, low, _ = call(
        last_kernel,
        "fit_last",
        [((4, 256, 128), F32), ((6, 256, 128), F32), pieced, pieced, ((256, 256), F32)],
        [SMEM] + [VMEM] * 25,
        place, *chunks, *pieces, *t,
    )
    highs, lows = highs + [high], lows + [low]
    got = swapped(send, "core")
    kept = added(keep, got)
    ladder_own, ladder_other = send, got
    for iteration in range(ITERS):
        last = iteration == ITERS - 1
        (start,) = call(
            lambda *refs: ladder_kernel(4, *refs),
            "ladder",
            [((4, 256, 256), F32)],
            [VMEM] * 4,
            driver, amps, ladder_own, ladder_other,
        )
        kept, other = summed(kept, start)
        (start,) = call(
            kept_kernel,
            "kept",
            [((4, 256, 256), F32)],
            [SMEM] + [VMEM] * 18,
            place, kept, start, *highs, *lows,
        )
        outs = [((4, 256, 256), F32)] + ([] if last else [((4, 256, 128), F32), whole, whole])
        amps, *rest = call(
            lambda *refs: step_kernel(last, *refs),
            "step",
            outs,
            [SMEM] + [VMEM] * 19,
            place, below, other, start, *highs, *lows,
        )
        if not last:
            send, *t = rest
            got = swapped(send, "core")
            (keep,) = call(
                keep_kernel,
                "keep",
                [((4, 256, 128), F32)],
                [SMEM] + [VMEM] * 18,
                place, *t, *highs, *lows,
            )
            kept = added(keep, got)
    return amps[None]


def solution(mesh):
    torus = Mesh(mesh.devices.reshape(4, 8, 2, 4, 2), AXES)
    in_specs = (
        P(WIDE, NARROW, None, None),
        P(WIDE, NARROW, None, None),
        P(NARROW, WIDE, None),
        P(None, WIDE, None),
        P(WIDE),
        P(NARROW),
        P(),
    )
    out_specs = P(WIDE, NARROW, None, None)
    return jax.shard_map(local, mesh=torus, in_specs=in_specs, out_specs=out_specs, check_vma=False)
```

```python
import jax
import jax.numpy as jnp
from jax import lax
from jax.experimental import pallas as pl
from jax.experimental.pallas import tpu as pltpu
from jax.sharding import Mesh
from jax.sharding import PartitionSpec as P


ITERS = 2
AXES = ("y_lo", "z", "y_hi", "x", "core")
WIDE = ("y_lo", "z")
NARROW = ("y_hi", "x", "core")
F32, BF16 = jnp.float32, jnp.bfloat16
VMEM = pl.BlockSpec(memory_space=pltpu.VMEM)
SMEM = pl.BlockSpec(memory_space=pltpu.SMEM)
ROWS = 136
PAIR = 272
ORDER = (0, 1, 2, 3, 7, 4, 5, 6)
NT = (((1,), (1,)), ((), ()))
NN = (((1,), (0,)), ((), ()))


def call(kernel, outs, in_specs, *operands, scratch=()):
    return pl.pallas_call(
        kernel,
        out_shape=[jax.ShapeDtypeStruct(s, d) for s, d in outs],
        in_specs=in_specs,
        out_specs=[VMEM] * len(outs),
        scratch_shapes=scratch,
        compiler_params=pltpu.CompilerParams(vmem_limit_bytes=8 << 20),
    )(*operands)


def split(value):
    high = value.astype(BF16)
    return high, (value - high.astype(F32)).astype(BF16)


def joined(pieces, axis):
    return pieces[0] if len(pieces) == 1 else jnp.concatenate(pieces, axis=axis)


def dot3(a, b, dims):
    (a0, a1), (b0, b1) = a, b
    left = joined([a0, a0, a1], 1)
    right = joined([b0, b1, b0], 1 if dims == NT else 0)
    return lax.dot_general(left, right, dims, preferred_element_type=F32)


def own_kernel(place, fit, factors, out, sems):
    copies = [
        pltpu.make_async_copy(fit.at[k], out.at[pl.ds(32 * k, 32)], sems.at[k]) for k in range(4)
    ]
    copies.append(
        pltpu.make_async_copy(factors.at[place[2]], out.at[pl.ds(128, 8)], sems.at[4])
    )
    for copy in copies:
        copy.start()
    for copy in copies:
        copy.wait()


def add_kernel(one, two, out):
    out[...] = one[...] + two[: one.shape[0]]


def total_kernel(parts, out):
    out[...] = (parts[0] + parts[1]) + (parts[2] + parts[3])


def copies_kernel(one, two, _, out):
    total = one[...] + two[...]
    for n in range(4):
        out[n] = total


def pack_kernel(one, two, out):
    for c, column in enumerate((one, two)):
        for k in range(4):
            at = 64 * k + 32 * c
            out[at : at + 32] = column[32 * k : 32 * (k + 1)]
        out[256 + 8 * c : 264 + 8 * c] = column[128:]


def early_kernel(row, occupied, amps, virtual, high, low, below):
    across = jnp.broadcast_to(virtual[...], (256, 256))
    pair = jnp.transpose(across) + across
    for k in range(4):
        high[k], low[k] = split(amps[k])
        below[k] = pair - row[0] - occupied[k]


def fit_chunk(amps, near, beyond, high, low):
    for k in range(4):
        at = slice(64 * k, 64 * (k + 1))
        high[k], low[k] = split(jnp.concatenate([near[at], beyond[at]], axis=0))
    a = tuple(joined([ref[k] for k in range(4)], 1) for ref in amps)
    b = tuple(joined([ref[k] for k in range(4)], 1) for ref in (high, low))
    return dot3(a, b, NT)


def fit_kernel(n, *refs):
    chunks, amps, outs = refs[: 2 * n], refs[2 * n : 2 * n + 2], refs[2 * n + 2 :]
    for c in range(n):
        outs[c][...] = fit_chunk(
            amps, chunks[2 * c], chunks[2 * c + 1], outs[n + c], outs[2 * n + c]
        )


def last_kernel(place, *refs):
    chunks, pieces, amps = refs[:16], refs[16:23], refs[23:25]
    keep, send, high, low, ladder = refs[25:]
    far = fit_chunk(amps, chunks[14], chunks[15], high, low)
    own = pieces[0][...]
    first = place[2] == 0
    keep[0] = jnp.where(first, own, far)
    send[0] = jnp.where(first, far, own)
    for n in range(3):
        below, above = pieces[1 + n][...], pieces[4 + n][...]
        keep[1 + n] = jnp.where(first, below, above)
        send[1 + n] = jnp.where(first, above, below)
    for n, step in enumerate((0, -1, -2, -3, 1, 2, 3, 4)):
        z = lax.rem(place[1] + 8 + step, 8)
        for s in range(4):
            y = lax.rem(place[0] + s, 4)
            at = 256 + 8 * (s % 2)
            rows = chunks[2 * n + s // 2][at : at + 8]
            ladder[pl.ds(pl.multiple_of((8 * y + z) * 8, 8), 8)] = rows
    send[4] = ladder[:, :128]
    send[5] = ladder[:, 128:]


def ladder_kernel(n, start, amps, own, other, out):
    factors = [split(jnp.concatenate([ref[n], ref[n + 1]], axis=1)) for ref in (own, other)]
    stack = tuple(joined([f[i] for f in factors], 0) for i in range(2))
    wide = tuple(joined([f[i] for f in factors], 1) for i in range(2))
    for j in range(4):
        left = dot3(stack, split(amps[j]), NN)
        left = split(jnp.concatenate([left[:256], left[256:]], axis=1))
        out[j] = start[j] + dot3(left, wide, NT)


def by_core(place, body):
    @pl.when(place[2] == 0)
    def _():
        body(ORDER)

    @pl.when(place[2] != 0)
    def _():
        body(ORDER[4:] + ORDER[:4])


def cycle_half(pieces, highs, lows, chosen, j):
    fit = tuple(joined([group[m][j] for m in chosen], 0) for group in (highs, lows))
    return dot3(pieces, fit, NN)


def fitted_half(amps, highs, lows, chosen, out):
    for n in (0, 2):
        fit = []
        for group in (highs, lows):
            two = [joined([group[m][k] for k in range(4)], 1) for m in chosen[n : n + 2]]
            fit.append(jnp.concatenate(two, axis=0))
        piece = dot3(amps, fit, NT)
        out[n], out[n + 1] = piece[:, :128], piece[:, 128:]


def side_by_side(ref):
    return jnp.concatenate([ref[n] for n in range(4)], axis=1)


def kept_kernel(place, kept, start, *refs):
    highs, lows, out = refs[:8], refs[8:16], refs[16]

    def body(order):
        pieces = split(side_by_side(kept))
        for j in range(4):
            out[j] = start[j] + cycle_half(pieces, highs, lows, order[:4], j)

    by_core(place, body)


def step_kernel(last, place, below, other, start, *refs):
    highs, lows = refs[:8], refs[8:16]
    current, *outs = refs[16:]

    def body(order):
        pieces = split(side_by_side(other))
        for j in range(4):
            cycle = cycle_half(pieces, highs, lows, order[4:], j)
            current[j] = (start[j] + cycle) / below[j]
        if last:
            return
        send, high, low = outs
        for k in range(4):
            high[k], low[k] = split(current[k])
        amps = tuple(joined([ref[k] for k in range(4)], 1) for ref in (high, low))
        fitted_half(amps, highs, lows, order[4:], send)

    by_core(place, body)


def keep_kernel(place, high, low, *refs):
    highs, lows, keep = refs[:8], refs[8:16], refs[16]

    def body(order):
        amps = tuple(joined([ref[k] for k in range(4)], 1) for ref in (high, low))
        fitted_half(amps, highs, lows, order[:4], keep)

    by_core(place, body)


def shifted(n, step):
    return [(i, (i + step) % n) for i in range(n)]


def along_z(shard, step):
    return lax.ppermute(shard, "z", shifted(8, step))


def swapped(shard, axis):
    return lax.ppermute(shard, axis, [(0, 1), (1, 0)])


def added(one, two):
    return call(add_kernel, [(one.shape, F32)], [VMEM] * 2, one, two)[0]


def summed(half, first):
    arrived = lax.all_to_all(half, "x", 0, 0, tiled=True)
    (piece,) = call(total_kernel, [(half.shape[1:], F32)], [VMEM], arrived)
    other = swapped(piece, "y_hi")
    (copies,) = call(copies_kernel, [(half.shape, F32)], [VMEM] * 3, piece, other, first)
    kept = lax.all_to_all(copies, "x", 0, 0, tiled=True)
    return kept, swapped(kept, "core")


def local(
    amplitudes, driver, fit_vectors, ladder_factors, row_energy, occupied_energy, virtual_energy
):
    amps, driver = amplitudes[0], driver[0]
    core = lax.axis_index("core")
    place = jnp.stack([lax.axis_index("y_lo"), lax.axis_index("z"), core]).astype(jnp.int32)
    (mine,) = call(
        own_kernel,
        [((ROWS, 256), F32)],
        [SMEM] + [pl.BlockSpec(memory_space=pltpu.HBM)] * 2,
        place,
        pltpu.with_memory_space_constraint(fit_vectors, pltpu.HBM),
        pltpu.with_memory_space_constraint(ladder_factors, pltpu.HBM),
        scratch=[pltpu.SemaphoreType.DMA((5,))],
    )
    columns = [mine] + [lax.ppermute(mine, "y_lo", shifted(4, s)) for s in (3, 2, 1)]
    whole, pieced = ((4, 256, 256), BF16), ((4, 128, 256), BF16)
    near, beyond = (
        call(pack_kernel, [((PAIR, 256), F32)], [VMEM] * 2, *columns[n : n + 2])[0]
        for n in (0, 2)
    )
    *t, below = call(
        early_kernel,
        [whole, whole, ((4, 256, 256), F32)],
        [SMEM] * 2 + [VMEM] * 2,
        row_energy, occupied_energy, amps, virtual_energy.reshape(1, 256),
    )

    def fits(*chunks):
        n = len(chunks)
        outs = [((256, 128), F32)] * n + [pieced] * (2 * n)
        flat = [half for chunk in chunks for half in chunk]
        got = call(lambda *refs: fit_kernel(n, *refs), outs, [VMEM] * (2 * n + 2), *flat, *t)
        return got[:n], got[n : 2 * n], got[2 * n :]

    up, down, found = [(near, beyond)], [(near, beyond)], [fits((near, beyond))]
    for _ in range(3):
        rising, falling = [], []
        for half in range(2):
            rising.append(along_z(up[-1][half], 1))
            falling.append(along_z(down[-1][half], -1))
        up.append(rising)
        down.append(falling)
        found.append(fits(up[-1], down[-1]))
    far = [along_z(up[-1][0], 1), along_z(down[-1][1], -1)]
    pieces, highs, lows = (
        [found[0][i][0]] + [f[i][0] for f in found[1:]] + [f[i][1] for f in found[1:]]
        for i in range(3)
    )
    chunks = [half for chunk in up + down[1:] + [far] for half in chunk]
    keep, send, high, low, _ = call(
        last_kernel,
        [((4, 256, 128), F32), ((6, 256, 128), F32), pieced, pieced, ((256, 256), F32)],
        [SMEM] + [VMEM] * 25,
        place, *chunks, *pieces, *t,
    )
    highs, lows = highs + [high], lows + [low]
    got = swapped(send, "core")
    kept = added(keep, got)
    ladder_own, ladder_other = send, got
    for iteration in range(ITERS):
        last = iteration == ITERS - 1
        (start,) = call(
            lambda *refs: ladder_kernel(4, *refs),
            [((4, 256, 256), F32)],
            [VMEM] * 4,
            driver, amps, ladder_own, ladder_other,
        )
        kept, other = summed(kept, start)
        (start,) = call(
            kept_kernel,
            [((4, 256, 256), F32)],
            [SMEM] + [VMEM] * 18,
            place, kept, start, *highs, *lows,
        )
        outs = [((4, 256, 256), F32)] + ([] if last else [((4, 256, 128), F32), whole, whole])
        amps, *rest = call(
            lambda *refs: step_kernel(last, *refs),
            outs,
            [SMEM] + [VMEM] * 19,
            place, below, other, start, *highs, *lows,
        )
        if not last:
            send, *t = rest
            got = swapped(send, "core")
            (keep,) = call(
                keep_kernel,
                [((4, 256, 128), F32)],
                [SMEM] + [VMEM] * 18,
                place, *t, *highs, *lows,
            )
            kept = added(keep, got)
    return amps[None]


def solution(mesh):
    torus = Mesh(mesh.devices.reshape(4, 8, 2, 4, 2), AXES)
    in_specs = (
        P(WIDE, NARROW, None, None),
        P(WIDE, NARROW, None, None),
        P(NARROW, WIDE, None),
        P(None, WIDE, None),
        P(WIDE),
        P(NARROW),
        P(),
    )
    out_specs = P(WIDE, NARROW, None, None)
    return jax.shard_map(local, mesh=torus, in_specs=in_specs, out_specs=out_specs, check_vma=False)
```
